512 devices in a mesh: axial: 64 (over x, z, core), radial: 8 (over y).
Axes of the slice: x: 4, y: 8, z: 8, core: 2. Of those that a mesh axis runs over, the one named last changes fastest.
Arguments:
- state_start: float32 [5, 640, 128, 128], P(None, 'axial', 'radial'), may hold values from -6 to 6
- forcing: float32 [640, 128, 128], P('axial', 'radial'), may hold values from -6 to 6
- signal: float32 [8], replicated, may hold values from -1 to 1
- mixing: float32 [2, 5, 5], replicated, may hold values from -0.4 to 0.4
- panel_cell: int32 [64, 8, 64, 4], P('axial', 'radial'), may hold values from -1 to 20479, as said below
- amplitude: float32 [64, 8, 64, 4, 512], P('axial', 'radial'), may hold values from -0.015625 to 0.015625
- delay: float32 [64, 8, 64, 4, 512], P('axial', 'radial'), may hold values from 0 to 8
- observer_list: int32 [512], replicated, may hold values from 0 to 511, each once
Outputs:
- final_state: float32 [5, 640, 128, 128], P(None, 'axial', 'radial')
- spectra: float32 [2, 4, 512], P(None, None, ('axial', 'radial'))
- adjoint_state: float32 [5, 640, 128, 128], P(None, 'axial', 'radial')
- forcing_grad: float32 [640, 128, 128], P('axial', 'radial')
The draws below stay inside these ranges and needn't reach their ends.
Inputs may be any that keep to these rules, and one draw needn't show every extreme that they name: `panel_cell`: each entry is a cell index of the sending tile, of 20480 cells, or -1 for an empty slot; the live slots of one tile and owner come first; one owner in each draw receives 4 live slots from every tile, and the largest cell index is reached.
All inputs are finite; a program needn't handle non-finite values.
Results may differ from the reference program's by a relative error of at most 0.0003.
Values sent between devices are 32-bit elements; how exact they have to be, the bound alone decides.
A program may use at most 128 MiB of HBM per device.

```python
import math
import jax
import jax.numpy as jnp
from jax import lax

FIELDS = 5
CX = 10
CR = 16
CT = 128
STEPS = 8
FREQ = 4
CAP = 4
TILES_A = 64
TILES_R = 8
OWNERS = 64
NX = 640
NR = 128
OBS = 512


def draw_panel_cell(key, part):
    count_key = jax.random.fold_in(key, 11)
    cell_key = jax.random.fold_in(key, 12)
    full_key = jax.random.fold_in(key, 13)
    counts = jax.random.randint(count_key, (TILES_A, TILES_R, OWNERS), 0, CAP + 1)
    busiest = jax.random.randint(full_key, (), 0, OWNERS)
    owner_ids = jnp.arange(OWNERS, dtype=jnp.int32)
    counts = jnp.where(owner_ids[None, None, :] == busiest, CAP, counts)
    cell_ids = jax.random.randint(cell_key, (TILES_A, TILES_R, OWNERS, CAP), 0, CX * CR * CT)
    cell_ids = cell_ids.at[0, 0, busiest, 0].set(CX * CR * CT - 1)
    slot_ids = jnp.arange(CAP, dtype=jnp.int32)
    return jnp.where(slot_ids[None, None, None, :] < counts[..., None], cell_ids, -1).astype(jnp.int32)


def block_scale(rng, shape, cuts, smallest, top_value):
    loudness, own = 1.0, jax.random.fold_in(rng, 6)
    for axis_at, blocks in cuts:
        steps = jnp.exp(jax.random.uniform(jax.random.fold_in(own, axis_at), (blocks,), jnp.float32, smallest / len(cuts), top_value / len(cuts)))
        loudness = loudness * jnp.repeat(steps, shape[axis_at] // blocks).reshape([-1 if axis == axis_at else 1 for axis in range(len(shape))])
    return loudness


def centred(own_key, dims, spread, most, cuts=(), held_as=jnp.bfloat16):
    loudness = block_scale(own_key, dims, cuts, -0.22, 0.18) if cuts else 1.0
    result = jax.random.normal(own_key, dims, jnp.float32) * spread * loudness
    return jnp.minimum(jnp.maximum(result, -most), most).astype(held_as)


def setup_inputs(seed: int = 0) -> dict:
    splits = jax.random.split(jax.random.key(seed), 9)
    state_start = centred(splits[0], (FIELDS, NX, NR, CT), 1.0, 6.0, ((1, 64), (2, 8)), jnp.float32)
    forcing = centred(splits[1], (NX, NR, CT), 1.0, 6.0, ((0, 64), (1, 8)), jnp.float32)
    signal = jnp.clip(jax.random.uniform(splits[2], (STEPS,), jnp.float32, -1.0, 1.0), -1.0, 1.0)
    mixing = centred(splits[3], (2, FIELDS, FIELDS), 0.1, 0.4, (), jnp.float32)
    panel_cell = draw_panel_cell(jax.random.fold_in(splits[8], 71), 0)
    amplitude = centred(splits[5], (TILES_A, TILES_R, OWNERS, CAP, OBS), (TILES_A * TILES_R * OWNERS * CAP) ** -0.5, 0.015625, ((0, 64), (1, 8)), jnp.float32)
    delay = jnp.clip(8.0 * jax.random.uniform(splits[6], (TILES_A, TILES_R, OWNERS, CAP, OBS), jnp.float32) ** block_scale(splits[6], (TILES_A, TILES_R, OWNERS, CAP, OBS), ((0, 64), (1, 8)), -0.2, 0.2), 0.0, 8.0)
    observer_list = jax.random.permutation(splits[7], OBS).astype(jnp.int32)
    return dict(state_start=state_start, forcing=forcing, signal=signal, mixing=mixing, panel_cell=panel_cell, amplitude=amplitude, delay=delay, observer_list=observer_list)


deriv_coef = (5.0 / 6.0, -5.0 / 21.0, 5.0 / 84.0, -5.0 / 504.0, 1.0 / 1260.0)
filter_coef = tuple(((-1.0) ** abs(offset)) * math.comb(10, 5 + offset) / 1024.0 for offset in range(-5, 6))
damping = 0.2
highest = lax.Precision.HIGHEST


def advance(padded, mixing, adjoint):
    span_x = padded.shape[1] - 10
    span_r = padded.shape[2] - 10
    count = padded.shape[0]

    def along_x(offset):
        return padded[:, 5 + offset:5 + offset + span_x, 5:5 + span_r, :]

    def along_r(offset):
        return padded[:, 5:5 + span_x, 5 + offset:5 + offset + span_r, :]

    centre = along_x(0)
    deriv_x = sum(deriv_coef[order] * (along_x(order + 1) - along_x(-order - 1)) for order in range(5))
    deriv_r = sum(deriv_coef[order] * (along_r(order + 1) - along_r(-order - 1)) for order in range(5))
    smooth = sum(filter_coef[offset + 5] * (along_x(offset) + along_r(offset)) for offset in range(-5, 6))
    factor = 1.0 if adjoint else -1.0
    outputs = []
    for target in range(count):
        term = centre[target] - damping * smooth[target]
        for source in range(count):
            if adjoint:
                coef_x = mixing[0, source, target]
                coef_r = mixing[1, source, target]
            else:
                coef_x = mixing[0, target, source]
                coef_r = mixing[1, target, source]
            term = term + factor * (coef_x * deriv_x[source] + coef_r * deriv_r[source])
        outputs.append(term)
    return jnp.stack(outputs)


def operator(field, mixing, adjoint):
    return advance(jnp.pad(field, ((0, 0), (5, 5), (5, 5), (0, 0))), mixing, adjoint)


def frequencies():
    return 2.0 * jnp.pi * (jnp.arange(FREQ, dtype=jnp.float32) + 1.0) / STEPS


def time_tables():
    levels = jnp.arange(STEPS, dtype=jnp.float32)
    phase = levels[:, None] * frequencies()[None, :]
    return jnp.cos(phase), jnp.sin(phase)


def panel_kernels(amp, lag):
    phase = frequencies()[None, :, None] * lag[:, None, :]
    return amp[:, None, :] * jnp.cos(phase), -amp[:, None, :] * jnp.sin(phase)


def partial_spectra(panels, kern_re, kern_im, cos_t, sin_t):
    coef_re = jnp.dot(panels, cos_t, precision=highest)
    coef_im = -jnp.dot(panels, sin_t, precision=highest)
    spec_re = jnp.einsum("pfo,pf->fo", kern_re, coef_re, precision=highest) - jnp.einsum("pfo,pf->fo", kern_im, coef_im, precision=highest)
    spec_im = jnp.einsum("pfo,pf->fo", kern_re, coef_im, precision=highest) + jnp.einsum("pfo,pf->fo", kern_im, coef_re, precision=highest)
    return jnp.stack([spec_re, spec_im])


def panel_sources(spectra, kern_re, kern_im, cos_t, sin_t):
    back_re = jnp.einsum("pfo,fo->pf", kern_re, spectra[0], precision=highest) + jnp.einsum("pfo,fo->pf", kern_im, spectra[1], precision=highest)
    back_im = jnp.einsum("pfo,fo->pf", kern_im, spectra[0], precision=highest) - jnp.einsum("pfo,fo->pf", kern_re, spectra[1], precision=highest)
    return 2.0 * (jnp.dot(back_re, cos_t.T, precision=highest) + jnp.dot(back_im, sin_t.T, precision=highest))


def tile_view(pressure):
    return pressure.reshape(TILES_A, CX, TILES_R, CR, CT).transpose(0, 2, 1, 3, 4).reshape(TILES_A, TILES_R, CX * CR * CT)


def panel_values(pressure, panel_cell):
    tiles = tile_view(pressure)
    clipped = jnp.maximum(panel_cell, 0).reshape(TILES_A, TILES_R, OWNERS * CAP).astype(jnp.int32)
    picked = jnp.take_along_axis(tiles, clipped, axis=2).reshape(panel_cell.shape)
    return jnp.where(panel_cell >= 0, picked, 0.0)


def inject(values, panel_cell):
    cell_total = CX * CR * CT
    targets = jnp.where(panel_cell >= 0, panel_cell, cell_total).reshape(TILES_A, TILES_R, OWNERS * CAP).astype(jnp.int32)
    axial_ids = jnp.arange(TILES_A, dtype=jnp.int32)[:, None, None]
    radial_ids = jnp.arange(TILES_R, dtype=jnp.int32)[None, :, None]
    flattened = jnp.zeros((TILES_A, TILES_R, cell_total), jnp.float32)
    flattened = flattened.at[axial_ids, radial_ids, targets].add(values.reshape(TILES_A, TILES_R, OWNERS * CAP), mode="drop")
    return flattened.reshape(TILES_A, TILES_R, CX, CR, CT).transpose(0, 2, 1, 3, 4).reshape(NX, NR, CT)


def reference(state_start, forcing, signal, mixing, panel_cell, amplitude, delay, observer_list):
    state = state_start
    records = []
    for level in range(STEPS):
        state = operator(state, mixing, False)
        state = state.at[4].add(signal[level] * forcing)
        records.append(panel_values(state[4], panel_cell))
    recorded = jnp.stack(records, axis=-1)
    owner_view = jnp.transpose(recorded, (2, 1, 0, 3, 4))
    chosen_amp = jnp.take(amplitude, observer_list, axis=4)
    chosen_lag = jnp.take(delay, observer_list, axis=4)
    cos_t, sin_t = time_tables()

    def owner_partial(items):
        panels, amp, lag = items
        kern_re, kern_im = panel_kernels(amp.reshape(-1, OBS), lag.reshape(-1, OBS))
        return partial_spectra(panels.reshape(-1, STEPS), kern_re, kern_im, cos_t, sin_t)

    spectra = jnp.sum(lax.map(owner_partial, (owner_view, chosen_amp, chosen_lag)), axis=0)

    def owner_sources(items):
        panels, amp, lag = items
        kern_re, kern_im = panel_kernels(amp.reshape(-1, OBS), lag.reshape(-1, OBS))
        return panel_sources(spectra, kern_re, kern_im, cos_t, sin_t).reshape(panels.shape)

    sources = lax.map(owner_sources, (owner_view, chosen_amp, chosen_lag))
    tile_sources = jnp.transpose(sources, (2, 1, 0, 3, 4))
    adjoint = jnp.zeros_like(state_start)
    gradient = jnp.zeros_like(forcing)
    for level in reversed(range(STEPS)):
        carried = adjoint.at[4].add(inject(tile_sources[..., level], panel_cell))
        gradient = gradient + signal[level] * carried[4]
        adjoint = operator(carried, mixing, True)
    return state, spectra, adjoint, gradient
```

```python
import functools
import math

import jax
import jax.numpy as jnp
from jax import lax
from jax.experimental import pallas as pl
from jax.experimental.pallas import tpu as pltpu
from jax.sharding import PartitionSpec as P

STEPS = 8
FREQ = 4


deriv_coef = (5.0 / 6.0, -5.0 / 21.0, 5.0 / 84.0, -5.0 / 504.0, 1.0 / 1260.0)
filter_coef = tuple(
    ((-1.0) ** abs(offset) * math.comb(10, 5 + offset) / 1024.0 for offset in range(-5, 6))
)
damping = 0.2
highest = lax.Precision.HIGHEST


def extended(block, sides, width):
    for axis, dim in sides:
        count = lax.axis_size(axis)
        forward = [(i, i + 1) for i in range(count - 1)]
        backward = [(target, source) for source, target in forward]
        low = lax.ppermute(
            lax.slice_in_dim(block, block.shape[dim] - width, None, axis=dim), axis, forward
        )
        high = lax.ppermute(lax.slice_in_dim(block, 0, width, axis=dim), axis, backward)
        block = jnp.concatenate([low, block, high], axis=dim)
    return block


def advance(padded, mixing, adjoint):
    span_x = padded.shape[1] - 10
    span_r = padded.shape[2] - 10
    count = padded.shape[0]

    def along_x(offset):
        return padded[:, 5 + offset : 5 + offset + span_x, 5 : 5 + span_r, :]

    def along_r(offset):
        return padded[:, 5 : 5 + span_x, 5 + offset : 5 + offset + span_r, :]

    centre = along_x(0)
    deriv_x = sum(
        (deriv_coef[order] * (along_x(order + 1) - along_x(-order - 1)) for order in range(5))
    )
    deriv_r = sum(
        (deriv_coef[order] * (along_r(order + 1) - along_r(-order - 1)) for order in range(5))
    )
    smooth = sum(
        (filter_coef[offset + 5] * (along_x(offset) + along_r(offset)) for offset in range(-5, 6))
    )
    factor = 1.0 if adjoint else -1.0
    outputs = []
    for target in range(count):
        term = centre[target] - damping * smooth[target]
        for source in range(count):
            if adjoint:
                coef_x = mixing[0, source, target]
                coef_r = mixing[1, source, target]
            else:
                coef_x = mixing[0, target, source]
                coef_r = mixing[1, target, source]
            term = term + factor * (coef_x * deriv_x[source] + coef_r * deriv_r[source])
        outputs.append(term)
    return jnp.stack(outputs)


HALO = 5


def neighbour_halos(block):
    axial = lax.axis_size("axial")
    radial = lax.axis_size("radial")
    up_a = [(i, i + 1) for i in range(axial - 1)]
    down_a = [(i + 1, i) for i in range(axial - 1)]
    up_r = [(i, i + 1) for i in range(radial - 1)]
    down_r = [(i + 1, i) for i in range(radial - 1)]
    rows = block.shape[1]
    cols = block.shape[2]
    x_low = lax.ppermute(block[:, rows - HALO :], "axial", up_a)
    x_high = lax.ppermute(block[:, :HALO], "axial", down_a)
    r_low = lax.ppermute(block[:, :, cols - HALO :], "radial", up_r)
    r_high = lax.ppermute(block[:, :, :HALO], "radial", down_r)
    return x_low, x_high, r_low, r_high


def step_kernel(with_extra, coef, block, x_low, x_high, r_low, r_high, *rest):
    if with_extra:
        extra, out, ext_r = rest
    else:
        out, ext_r = rest
    count, rows, cols, _ = block.shape
    top = 8
    for s in range(count):
        ext_r[s, :, top - HALO : top, :] = r_low[s]
        ext_r[s, :, top : top + cols, :] = block[s]
        ext_r[s, :, top + cols : top + cols + HALO, :] = r_high[s]
    cx = [[coef[t * count + s] for s in range(count)] for t in range(count)]
    cr = [[coef[count * count + t * count + s] for s in range(count)] for t in range(count)]
    for i in range(rows):
        acc = [None] * count
        for s in range(count):

            def along_x(k):
                j = i + k
                if j < 0:
                    return x_low[s, HALO + j]
                if j >= rows:
                    return x_high[s, j - rows]
                return block[s, j]

            def along_r(k):
                return ext_r[s, i, top + k : top + k + cols, :]

            centre = block[s, i]
            dx = None
            dr = None
            smooth = filter_coef[HALO] * (centre + centre)
            for o in range(1, HALO + 1):
                xp, xm = along_x(o), along_x(-o)
                rp, rm = along_r(o), along_r(-o)
                tx = deriv_coef[o - 1] * (xp - xm)
                tr = deriv_coef[o - 1] * (rp - rm)
                dx = tx if dx is None else dx + tx
                dr = tr if dr is None else dr + tr
                smooth = smooth + filter_coef[HALO + o] * ((xp + xm) + (rp + rm))
            for t in range(count):
                term = cx[t][s] * dx + cr[t][s] * dr
                if t == s:
                    term = term + (centre - damping * smooth)
                acc[t] = term if acc[t] is None else acc[t] + term
        for t in range(count):
            value = acc[t]
            if with_extra and t == count - 1:
                value = value + coef[2 * count * count] * extra[i]
            out[t, i] = value


def stencil_step(block, mixing_x, mixing_r, scale=None, extra=None):
    count, rows, cols, lanes = block.shape
    halos = neighbour_halos(block)
    with_extra = extra is not None
    pieces = [mixing_x.reshape(-1), mixing_r.reshape(-1)]
    if with_extra:
        pieces.append(jnp.reshape(scale, (1,)))
    coef = jnp.concatenate(pieces)
    args = [coef, block, *halos] + ([extra] if with_extra else [])
    vmem = pl.BlockSpec(memory_space=pltpu.VMEM)
    cells = count * rows * cols * lanes
    return pl.pallas_call(
        functools.partial(step_kernel, with_extra),
        out_shape=jax.ShapeDtypeStruct(block.shape, jnp.float32),
        in_specs=[pl.BlockSpec(memory_space=pltpu.SMEM)] + [vmem] * (len(args) - 1),
        out_specs=vmem,
        scratch_shapes=[pltpu.VMEM((count, rows, cols + 16, lanes), jnp.float32)],
        cost_estimate=pl.CostEstimate(flops=80 * cells, bytes_accessed=16 * cells, transcendentals=0),
    )(*args)


def frequencies():
    return 2.0 * jnp.pi * (jnp.arange(FREQ, dtype=jnp.float32) + 1.0) / STEPS


def time_tables():
    levels = jnp.arange(STEPS, dtype=jnp.float32)
    phase = levels[:, None] * frequencies()[None, :]
    return (jnp.cos(phase), jnp.sin(phase))


def panel_kernels(amp, lag):
    phase = frequencies()[None, :, None] * lag[:, None, :]
    return (amp[:, None, :] * jnp.cos(phase), -amp[:, None, :] * jnp.sin(phase))


def partial_spectra(panels, kern_re, kern_im, cos_t, sin_t):
    coef_re = jnp.dot(panels, cos_t, precision=highest)
    coef_im = -jnp.dot(panels, sin_t, precision=highest)
    spec_re = jnp.einsum("pfo,pf->fo", kern_re, coef_re, precision=highest) - jnp.einsum(
        "pfo,pf->fo", kern_im, coef_im, precision=highest
    )
    spec_im = jnp.einsum("pfo,pf->fo", kern_re, coef_im, precision=highest) + jnp.einsum(
        "pfo,pf->fo", kern_im, coef_re, precision=highest
    )
    return jnp.stack([spec_re, spec_im])


def panel_sources(spectra, kern_re, kern_im, cos_t, sin_t):
    back_re = jnp.einsum("pfo,fo->pf", kern_re, spectra[0], precision=highest) + jnp.einsum(
        "pfo,fo->pf", kern_im, spectra[1], precision=highest
    )
    back_im = jnp.einsum("pfo,fo->pf", kern_im, spectra[0], precision=highest) - jnp.einsum(
        "pfo,fo->pf", kern_re, spectra[1], precision=highest
    )
    return 2.0 * (
        jnp.dot(back_re, cos_t.T, precision=highest) + jnp.dot(back_im, sin_t.T, precision=highest)
    )


def on_device(state_start, forcing, signal, mixing, panel_cell, amplitude, delay, observer_list):
    slots = panel_cell[0, 0]
    cell_total = forcing.shape[0] * forcing.shape[1] * forcing.shape[2]
    live = slots >= 0
    targets = jnp.where(live, slots, cell_total)
    clipped = jnp.minimum(targets, cell_total - 1)
    state = state_start
    records = []
    forward_x = -mixing[0]
    forward_r = -mixing[1]
    for level in range(STEPS):
        state = stencil_step(state, forward_x, forward_r, signal[level], forcing)
        records.append(jnp.where(live, jnp.take(state[4].reshape(-1), clipped), 0.0))
    stacked = jnp.stack(records, axis=-1)
    received = lax.all_to_all(stacked, "axial", split_axis=0, concat_axis=0, tiled=True)
    observers = observer_list.shape[0]
    chosen_amp = jnp.take(amplitude[0, 0], observer_list, axis=2).reshape(-1, observers)
    chosen_lag = jnp.take(delay[0, 0], observer_list, axis=2).reshape(-1, observers)
    kern_re, kern_im = panel_kernels(chosen_amp, chosen_lag)
    cos_t, sin_t = time_tables()
    partial_sum = partial_spectra(received.reshape(-1, STEPS), kern_re, kern_im, cos_t, sin_t)
    share = observers // lax.axis_size(("axial", "radial"))
    total = lax.psum(partial_sum, ("axial", "radial"))
    mine = lax.dynamic_slice_in_dim(total, lax.axis_index(("axial", "radial")) * share, share, 2)
    sources = panel_sources(total, kern_re, kern_im, cos_t, sin_t).reshape(received.shape)
    returned = lax.all_to_all(sources, "axial", split_axis=0, concat_axis=0, tiled=True)
    flat_targets = targets.reshape(-1)
    adjoint = jnp.zeros_like(state_start)
    gradient = jnp.zeros_like(forcing)
    for level in reversed(range(STEPS)):
        spread = (
            jnp.zeros((cell_total,), jnp.float32)
            .at[flat_targets]
            .add(returned[:, :, level].reshape(-1), mode="drop")
        )
        carried = adjoint.at[4].add(spread.reshape(forcing.shape))
        gradient = gradient + signal[level] * carried[4]
        adjoint = stencil_step(carried, mixing[0].T, mixing[1].T)
    return (state, mine, adjoint, gradient)


def solution(mesh):
    return jax.shard_map(
        on_device,
        mesh=mesh,
        in_specs=(
            P(None, "axial", "radial", None),
            P("axial", "radial", None),
            P(),
            P(),
            P("axial", "radial", None, None),
            P("axial", "radial", None, None, None),
            P("axial", "radial", None, None, None),
            P(),
        ),
        out_specs=(
            P(None, "axial", "radial", None),
            P(None, None, ("axial", "radial")),
            P(None, "axial", "radial", None),
            P("axial", "radial", None),
        ),
        check_vma=False,
    )
```
